32 devices in a mesh: segment: 4 (over y, x), seq: 8 (over z, core).
Axes of the slice: x: 2, y: 2, z: 4, core: 2. Of those that a mesh axis runs over, the one named last changes fastest.
Arguments:
- token_ids: int32 [64], P('seq'), may hold values from 0 to 511
- cached_len: int32 [2], replicated, may hold values from 128 to 786432
- embed: bfloat16 [512, 8192], P(None, 'seq'), may hold values from -6 to 6
- gain: float32 [4, 8192], P('segment'), may hold values from 0.1 to 1.9
- w_in: bfloat16 [4, 8192, 3, 8192], P('segment', None, None, 'seq'), may hold values from -0.0625 to 0.0625
- short_filter: float32 [4, 7, 3, 8192], P('segment', None, None, 'seq'), may hold values from -2.5 to 2.5
- long_filter: float32 [4, 128, 512], P('segment', None, 'seq'), may hold values from -0.5 to 0.5
- w_out: bfloat16 [4, 8192, 8192], P('segment', None, 'seq'), may hold values from -0.0625 to 0.0625
- short_cycle: bfloat16 [4, 2, 128, 3, 8192], P('segment', None, None, None, 'seq'), may hold values from -6 to 6
- long_cycle: bfloat16 [4, 2, 128, 8192], P('segment', None, None, 'seq'), may hold values from -6 to 6
Outputs:
- section_out: bfloat16 [4, 64, 8192], P('segment', None, 'seq')
- new_short_cycle: bfloat16 [4, 2, 128, 3, 8192], P('segment', None, None, None, 'seq')
- new_long_cycle: bfloat16 [4, 2, 128, 8192], P('segment', None, None, 'seq')
The draws below stay inside these ranges and needn't reach their ends.
All inputs are finite; a program needn't handle non-finite values.
Results may differ from the reference program's by a relative error of at most 0.023.
Values may be sent and summed in bfloat16 or wider, within the bound.
No kernel may reach another device: no remote copies, remote signals or barrier semaphores. Data moves between devices by JAX's collectives and lax.ppermute only.
A program may use at most 192 MiB of HBM per device.

```python
import math
import jax
import jax.numpy as jnp
import numpy as np
from jax import lax

D = 8192
G = 512
VOCAB = 512
SHORT = 7
LONG = 128
CONTEXT = 786432
REQUESTS = 2
TOKENS = 64
NEW = 32
LAYERS = 4


def plant(result, stream_key, low, largest):
    index_at = [jax.random.randint(jax.random.fold_in(stream_key, axis), (), 0, length) for axis, length in enumerate(result.shape)]
    main_axis = result.shape.index(max(result.shape))
    next_to = index_at[:main_axis] + [(index_at[main_axis] + 1) % result.shape[main_axis]] + index_at[main_axis + 1:]
    return result.at[tuple(index_at)].set(low).at[tuple(next_to)].set(largest)


def level_of(stream_key, shape, split, smallest, top_value):
    factor_of, own = 1.0, jax.random.fold_in(stream_key, 6)
    for axis_at, shards_of in split:
        heights = jnp.exp(jax.random.uniform(jax.random.fold_in(own, axis_at), (shards_of,), jnp.float32, smallest / len(split), top_value / len(split)))
        factor_of = factor_of * jnp.repeat(heights, shape[axis_at] // shards_of).reshape([-1 if axis == axis_at else 1 for axis in range(len(shape))])
    return factor_of


def cumulative_ranks(number_of, slope):
    weights = [(1 << 20) // math.isqrt(standing ** slope) + 1 for standing in range(1, number_of + 1)]
    width = 1 + sum(weights) // (1 << 30)
    return np.cumsum(np.array([max(1, weight // width) for weight in weights]))


def skewed_ids(own_key, extent, amount, skew):
    listing = cumulative_ranks(amount, skew)
    ticket = jax.random.randint(jax.random.fold_in(own_key, 1), extent, 0, int(listing[amount - 1]))
    grade = jnp.searchsorted(jnp.asarray(listing, jnp.int32), ticket, side="right")
    return jax.random.permutation(jax.random.fold_in(own_key, 2), amount)[grade].astype(jnp.int32)


def noise(stream_key, shape, spread, most, split=(), dtype=jnp.bfloat16):
    level = level_of(stream_key, shape, split, -0.22, 0.18) if split else 1.0
    array = jax.random.normal(stream_key, shape, jnp.float32) * spread * level
    return jnp.minimum(jnp.maximum(array, -most), most).astype(dtype)


def setup_inputs(seed: int = 0) -> dict:
    arg_keys = jax.random.split(jax.random.key(seed), 11)
    token_ids = plant(skewed_ids(arg_keys[0], (TOKENS,), VOCAB, 2), jax.random.fold_in(arg_keys[0], 3), 0, VOCAB - 1).astype(jnp.int32)
    cached_len = jax.random.randint(arg_keys[1], (REQUESTS,), LONG, CONTEXT + 1).astype(jnp.int32)
    embed = noise(arg_keys[2], (VOCAB, D), 1.0, 6.0, ((1, 8),))
    gain = jnp.clip(1.0 + 0.18 * jax.random.normal(arg_keys[3], (LAYERS, D), jnp.float32), 0.1, 1.9)
    w_in = noise(arg_keys[4], (LAYERS, D, 3, D), D ** -0.5, 0.0625, ((0, 4), (3, 8)))
    short_filter = noise(arg_keys[5], (LAYERS, SHORT, 3, D), 0.4, 2.5, ((0, 4), (3, 8)), jnp.float32)
    long_filter = noise(arg_keys[6], (LAYERS, LONG, G), 0.09, 0.5, ((0, 4), (2, 8)), jnp.float32)
    w_out = noise(arg_keys[7], (LAYERS, D, D), D ** -0.5, 0.0625, ((0, 4), (2, 8)))
    short_cycle = noise(arg_keys[8], (LAYERS, REQUESTS, LONG, 3, D), 1.0, 6.0, ((0, 4), (4, 8)))
    long_cycle = noise(arg_keys[9], (LAYERS, REQUESTS, LONG, D), 1.0, 6.0, ((0, 4), (3, 8)))
    return dict(token_ids=token_ids, cached_len=cached_len, embed=embed, gain=gain, w_in=w_in, short_filter=short_filter, long_filter=long_filter, w_out=w_out, short_cycle=short_cycle, long_cycle=long_cycle)


def cycle_rows(cycle, offset):
    doubled = jnp.concatenate([cycle, cycle], axis=0)
    return lax.dynamic_slice_in_dim(doubled, offset.astype(jnp.int32), cycle.shape[0], 0)

def reference(token_ids, cached_len, embed, gain, w_in, short_filter, long_filter, w_out, short_cycle, long_cycle):
    hidden = embed[token_ids]
    section_list = []
    short_list = []
    long_list = []
    for layer in range(LAYERS):
        widened = hidden.astype(jnp.float32)
        scaling = lax.rsqrt(lax.optimization_barrier(jnp.mean(widened * widened, axis=1, keepdims=True)) + 1e-06)
        normed = (widened * scaling * gain[layer][None, :]).astype(jnp.bfloat16)
        projected = jnp.dot(normed, w_in[layer].reshape(D, 3 * D), preferred_element_type=jnp.float32)
        projected = projected.astype(jnp.bfloat16).reshape(TOKENS, 3, D)
        channel_taps = jnp.repeat(long_filter[layer], D // G, axis=1)
        mixed_parts = []
        short_cycles = []
        long_cycles = []
        for request in range(REQUESTS):
            prefix = cached_len[request]
            appended = projected[request * NEW:(request + 1) * NEW]
            extended = jnp.concatenate([cycle_rows(short_cycle[layer, request], prefix % LONG), appended], axis=0)
            wide_ext = extended.astype(jnp.float32)
            filtered = jnp.zeros((NEW, 3, D), jnp.float32)
            for tap_index in range(SHORT):
                filtered = filtered + short_filter[layer, tap_index][None] * wide_ext[LONG - tap_index:LONG - tap_index + NEW]
            product = (filtered[:, 1] * filtered[:, 2]).astype(jnp.bfloat16)
            carried = jnp.concatenate([cycle_rows(long_cycle[layer, request], prefix % LONG), product], axis=0)
            wide_carried = carried.astype(jnp.float32)
            convolved = jnp.zeros((NEW, D), jnp.float32)
            for tap_index in range(LONG):
                convolved = convolved + channel_taps[tap_index][None] * wide_carried[LONG - tap_index:LONG - tap_index + NEW]
            mixed_parts.append((filtered[:, 0] * convolved).astype(jnp.bfloat16))
            backward = (LONG - (prefix + NEW) % LONG) % LONG
            short_cycles.append(cycle_rows(extended[NEW:], backward))
            long_cycles.append(cycle_rows(carried[NEW:], backward))
        mixed = jnp.concatenate(mixed_parts, axis=0)
        added = jnp.dot(mixed, w_out[layer], preferred_element_type=jnp.float32)
        hidden = (hidden.astype(jnp.float32) + added).astype(jnp.bfloat16)
        section_list.append(hidden)
        short_list.append(jnp.stack(short_cycles))
        long_list.append(jnp.stack(long_cycles))
    return (jnp.stack(section_list), jnp.stack(short_list), jnp.stack(long_list))
```

```python
import functools

import jax
import jax.numpy as jnp
from jax import lax
from jax.experimental import pallas as pl
from jax.experimental.pallas import tpu as pltpu
from jax.sharding import PartitionSpec as P

VOCAB = 512
LONG = 128
REQUESTS = 2
BRANCHES = 3
TAIL = 8
LANE = 128
EPS = 1e-06
MIB = 1 << 20


WHOLE = pl.BlockSpec(memory_space=pltpu.VMEM)


def mate(lane, step, lanes):
    return lane ^ step if lanes & (lanes - 1) == 0 else (lane - step) % lanes


def send_to(lane, step, lanes):
    return lane ^ step if lanes & (lanes - 1) == 0 else (lane + step) % lanes


def gather_step(block, step, source, target, lanes):
    n = 2 * lanes
    pairs = [
        (source * n + 2 * lane + core, target * n + 2 * send_to(lane, step, lanes) + core)
        for lane in range(lanes)
        for core in range(2)
    ]
    return lax.ppermute(block, ("segment", "seq"), pairs)


def other_core(block, segment, lanes):
    n = 2 * lanes
    pairs = [(segment * n + i, segment * n + (i ^ 1)) for i in range(n)]
    return lax.ppermute(block, ("segment", "seq"), pairs)


def pieces_of(blocks, segment, lanes):
    return [(block, other_core(block, segment, lanes)) for block in blocks]


def in_kernel(first, tab, xa, xb, gain, w, *rest):
    if first:
        acc, ssq, xg = rest
    else:
        acc_in, ssq_in, acc, ssq, xg = rest
    g = pl.program_id(0)
    branch = lax.rem(g, BRANCHES)

    def load(x_ref, fresh):
        x = x_ref[...].astype(jnp.float32)
        xg[...] = (x * gain[0]).astype(jnp.bfloat16)
        square = x * x
        total = square[:, :LANE]
        for i in range(1, square.shape[1] // LANE):
            total = total + square[:, i * LANE : (i + 1) * LANE]
        if fresh and first:
            ssq[...] = total
        elif fresh:
            ssq[...] = ssq_in[...] + total
        else:
            ssq[...] += total

    @pl.when(g == 0)
    def _():
        load(xa, True)

    @pl.when(g == BRANCHES)
    def _():
        load(xb, False)

    part = jnp.dot(xg[...], w[0], preferred_element_type=jnp.float32)

    @pl.when(g < BRANCHES)
    def _():
        if first:
            acc[branch] = part
        else:
            acc[branch] = acc_in[branch] + part

    @pl.when(g >= BRANCHES)
    def _():
        acc[branch] += part


def in_chunk(table, step, piece, gain, w, carry):
    xa, xb = piece
    tokens, channels = xa.shape
    first = carry is None
    args = [table, xa, xb, gain, w] + ([] if first else list(carry))
    w_spec = pl.BlockSpec(
        (1, channels, channels), lambda g, tab: (g % BRANCHES, tab[2 * step + g // BRANCHES], 0)
    )
    gain_spec = pl.BlockSpec((1, 1, channels), lambda g, tab: (tab[2 * step + g // BRANCHES], 0, 0))
    return pl.pallas_call(
        functools.partial(in_kernel, first),
        grid_spec=pltpu.PrefetchScalarGridSpec(
            num_scalar_prefetch=1,
            grid=(2 * BRANCHES,),
            in_specs=[WHOLE, WHOLE, gain_spec, w_spec] + ([] if first else [WHOLE, WHOLE]),
            out_specs=[WHOLE, WHOLE],
            scratch_shapes=[pltpu.VMEM((tokens, channels), jnp.bfloat16)],
        ),
        out_shape=[
            jax.ShapeDtypeStruct((BRANCHES, tokens, channels), jnp.float32),
            jax.ShapeDtypeStruct((tokens, LANE), jnp.float32),
        ],
        input_output_aliases={} if first else {5: 0, 6: 1},
        cost_estimate=pl.CostEstimate(
            flops=12 * tokens * channels * channels,
            bytes_accessed=12 * channels * channels,
            transcendentals=0,
        ),
        compiler_params=pltpu.CompilerParams(vmem_limit_bytes=12 * MIB),
        name="in_chunk",
    )(*args)


def mix_kernel(turn_at, width, tab, acc, ssq, sfilt, taps, cached, tails, proj_in, prod_in, mixed, proj, prod, ext, f0, pz):
    tokens, channels = mixed.shape
    appended = tokens // REQUESTS
    scale = lax.rsqrt(jnp.sum(ssq[...], axis=1, keepdims=True) / width + EPS)
    mine = tab[turn_at] != 0
    for b in range(BRANCHES):
        projected = (acc[b] * scale).astype(jnp.bfloat16)
        proj[b] = jnp.where(mine, projected, proj_in[b])
        wide = projected.astype(jnp.float32)
        for r in range(REQUESTS):
            ext[b, r, :TAIL] = tails[r, b]
            ext[b, r, TAIL:] = wide[r * appended : (r + 1) * appended]
    pz[:, :appended] = jnp.zeros((REQUESTS, appended, channels), jnp.float32)
    block = min(256, channels)
    short = sfilt.shape[0] // BRANCHES
    for r in range(REQUESTS):

        @pl.loop(0, channels // block)
        def _(i, r=r):
            cols = pl.ds(pl.multiple_of(i * block, block), block)
            rows = pl.ds(r * appended, appended)
            branches = []
            for b in range(BRANCHES):
                total = jnp.zeros((appended, block), jnp.float32)
                for j in range(short):
                    total = total + sfilt[j * BRANCHES + b, :, cols] * ext[b, r, pl.ds(TAIL - j, appended), cols]
                branches.append(total)
            product = (branches[1] * branches[2]).astype(jnp.bfloat16)
            pz[r, pl.ds(appended, appended), cols] = product.astype(jnp.float32)
            prod[rows, cols] = jnp.where(mine, product, prod_in[rows, cols])
            f0[rows, cols] = branches[0]

        @pl.loop(0, channels // block)
        def _(i, r=r):
            cols = pl.ds(pl.multiple_of(i * block, block), block)
            rows = pl.ds(r * appended, appended)
            total = cached[rows, cols]
            for j in range(min(appended, LONG)):
                total = total + taps[pl.ds(j, 1), cols] * pz[r, pl.ds(appended - j, appended), cols]
            mixed[rows, cols] = (f0[rows, cols] * total).astype(jnp.bfloat16)


def mix(table, turn_at, width, carry, sfilt, taps, cached, tails, proj, prod):
    tokens, channels = prod.shape
    appended = tokens // REQUESTS
    return pl.pallas_call(
        functools.partial(mix_kernel, turn_at, width),
        grid_spec=pltpu.PrefetchScalarGridSpec(
            num_scalar_prefetch=1,
            grid=(),
            in_specs=[WHOLE] * 8,
            out_specs=[WHOLE] * 3,
            scratch_shapes=[
                pltpu.VMEM((BRANCHES, REQUESTS, TAIL + appended, channels), jnp.float32),
                pltpu.VMEM((tokens, channels), jnp.float32),
                pltpu.VMEM((REQUESTS, 2 * appended, channels), jnp.float32),
            ],
        ),
        out_shape=[
            jax.ShapeDtypeStruct((tokens, channels), jnp.bfloat16),
            jax.ShapeDtypeStruct(proj.shape, jnp.bfloat16),
            jax.ShapeDtypeStruct(prod.shape, jnp.bfloat16),
        ],
        input_output_aliases={7: 1, 8: 2},
        cost_estimate=pl.CostEstimate(flops=80 * tokens * channels, bytes_accessed=24 * tokens * channels, transcendentals=0),
        compiler_params=pltpu.CompilerParams(vmem_limit_bytes=8 * MIB),
        name="mix",
    )(table, *carry, sfilt, taps, cached, tails, proj, prod)


def out_kernel(first, last, turn_at, tab, ma, mb, w, *rest):
    g = pl.program_id(0)
    if last:
        acc_in, current, result_in, out, result, acc = rest
    elif first:
        (acc,) = rest
    else:
        acc_in, acc = rest

    @pl.when(g == 0)
    def _():
        part = jnp.dot(ma[...], w[...], preferred_element_type=jnp.float32)
        acc[...] = part if first else acc_in[...] + part

    @pl.when(g == 1)
    def _():
        total = acc[...] + jnp.dot(mb[...], w[...], preferred_element_type=jnp.float32)
        if last:
            rows = (current[...].astype(jnp.float32) + total).astype(jnp.bfloat16)
            out[...] = rows
            result[...] = jnp.where(tab[turn_at] != 0, rows, result_in[...])
        else:
            acc[...] = total


def out_chunk(table, step, piece, w, acc, last=None, turn_at=0):
    ma, mb = piece
    tokens, channels = ma.shape
    first = acc is None
    args = [table, ma, mb, w] + ([] if first else [acc])
    wide = jax.ShapeDtypeStruct((tokens, channels), jnp.float32)
    slim = jax.ShapeDtypeStruct((tokens, channels), jnp.bfloat16)
    if last is not None:
        args += list(last)
        out_shape, aliases, scratch = [slim, slim], {6: 1}, [pltpu.VMEM((tokens, channels), jnp.float32)]
    else:
        out_shape, aliases, scratch = [wide], ({} if first else {4: 0}), []
    w_spec = pl.BlockSpec((channels, channels), lambda g, tab: (tab[2 * step + g], 0))
    result = pl.pallas_call(
        functools.partial(out_kernel, first, last is not None, turn_at),
        grid_spec=pltpu.PrefetchScalarGridSpec(
            num_scalar_prefetch=1,
            grid=(2,),
            in_specs=[WHOLE, WHOLE, w_spec] + [WHOLE] * (len(args) - 4),
            out_specs=[WHOLE] * len(out_shape),
            scratch_shapes=scratch,
        ),
        out_shape=out_shape,
        input_output_aliases=aliases,
        cost_estimate=pl.CostEstimate(
            flops=4 * tokens * channels * channels, bytes_accessed=4 * channels * channels, transcendentals=0
        ),
        compiler_params=pltpu.CompilerParams(vmem_limit_bytes=8 * MIB),
        name="out_chunk",
    )(*args)
    return result if last is not None else result[0]


def prep_kernel(lens, short, long, taps, cached, tails, ring):
    tokens, channels = cached.shape
    appended = tokens // REQUESTS
    block = min(256, channels)
    ring[LONG:] = jnp.zeros((appended, block), jnp.float32)
    for r in range(REQUESTS):
        start = lax.rem(LONG - lax.rem(lens[r], LONG), LONG)

        @pl.loop(0, channels // block)
        def _(i, r=r, start=start):
            cols = pl.ds(pl.multiple_of(i * block, block), block)
            for b in range(BRANCHES):
                tails[r, b, :, cols] = pltpu.roll(short[r, b, :, cols].astype(jnp.float32), start, 0)[LONG - TAIL :]
            ring[:LONG] = pltpu.roll(long[r, :, cols].astype(jnp.float32), start, 0)
            total = jnp.zeros((appended, block), jnp.float32)
            for j in range(1, LONG):
                total = total + taps[pl.ds(j, 1), cols] * ring[pl.ds(LONG - j, appended), :]
            cached[pl.ds(r * appended, appended), cols] = total


def prep(lens, short, long, taps, tokens):
    channels = long.shape[-1]
    appended = tokens // REQUESTS
    return pl.pallas_call(
        prep_kernel,
        in_specs=[pl.BlockSpec(memory_space=pltpu.SMEM), WHOLE, WHOLE, WHOLE],
        out_specs=[WHOLE, WHOLE],
        out_shape=[
            jax.ShapeDtypeStruct((tokens, channels), jnp.float32),
            jax.ShapeDtypeStruct((REQUESTS, BRANCHES, TAIL, channels), jnp.float32),
        ],
        scratch_shapes=[pltpu.VMEM((LONG + appended, min(256, channels)), jnp.float32)],
        cost_estimate=pl.CostEstimate(flops=256 * tokens * channels, bytes_accessed=20 * LONG * channels, transcendentals=0),
        compiler_params=pltpu.CompilerParams(vmem_limit_bytes=10 * MIB),
        name="prep",
    )(lens, short, long, taps)


def caches_kernel(lens, proj, prod, short, long, new_short, new_long, ring):
    tokens, channels = prod.shape
    appended = tokens // REQUESTS
    block = ring.shape[1]
    slots = lax.broadcasted_iota(jnp.int32, (LONG, block), 0)
    ring[...] = jnp.zeros((LONG, block), jnp.float32)
    for r in range(REQUESTS):
        at = lax.rem(lens[r], LONG)
        fresh = lax.rem(slots - at + LONG, LONG) < appended

        @pl.loop(0, channels // block)
        def _(i, r=r, at=at, fresh=fresh):
            cols = pl.ds(pl.multiple_of(i * block, block), block)
            rows = pl.ds(r * appended, appended)

            def replace(new, old):
                ring[:appended] = new.astype(jnp.float32)
                turned = pltpu.roll(ring[...], at, 0)
                return jnp.where(fresh, turned, old.astype(jnp.float32)).astype(jnp.bfloat16)

            for b in range(BRANCHES):
                new_short[r, b, :, cols] = replace(proj[b, rows, cols], short[r, b, :, cols])
            new_long[r, :, cols] = replace(prod[rows, cols], long[r, :, cols])


def caches(lens, proj, prod, short, long):
    channels = prod.shape[-1]
    return pl.pallas_call(
        caches_kernel,
        in_specs=[pl.BlockSpec(memory_space=pltpu.SMEM)] + [WHOLE] * 4,
        out_specs=[WHOLE, WHOLE],
        out_shape=[
            jax.ShapeDtypeStruct(short.shape, jnp.bfloat16),
            jax.ShapeDtypeStruct(long.shape, jnp.bfloat16),
        ],
        scratch_shapes=[pltpu.VMEM((LONG, min(256, channels)), jnp.float32)],
        cost_estimate=pl.CostEstimate(
            flops=8 * LONG * channels, bytes_accessed=32 * LONG * channels, transcendentals=0
        ),
        compiler_params=pltpu.CompilerParams(vmem_limit_bytes=10 * MIB),
        name="caches",
    )(lens, proj, prod, short, long)


def local(
    token_ids,
    cached_len,
    embed,
    gain,
    w_in,
    short_filter,
    long_filter,
    w_out,
    short_cycle,
    long_cycle,
):
    segments = lax.axis_size("segment")
    n = lax.axis_size("seq")
    lanes = n // 2
    own_tokens = token_ids.shape[0]
    tokens = own_tokens * n
    channels = embed.shape[1]
    width = gain.shape[1]
    my_segment = lax.axis_index("segment")
    me = lax.axis_index("seq")
    lane, core = me // 2, me % 2

    steps = jnp.arange(2 * lanes, dtype=jnp.int32)
    sources = 2 * mate(lane, steps // 2, lanes) + (core ^ (steps % 2))
    mine = (jnp.arange(segments, dtype=jnp.int32) == my_segment).astype(jnp.int32)
    table = jnp.concatenate([sources.astype(jnp.int32), mine])

    def swap(block):
        return lax.ppermute(block, "seq", [(i, i ^ 1) for i in range(n)])

    pair = jnp.stack([token_ids, swap(token_ids)])
    received = [pair]
    for step in range(1, lanes):
        pairs = [(2 * i + c, 2 * send_to(i, step, lanes) + c) for i in range(lanes) for c in range(2)]
        received.append(lax.ppermute(pair, "seq", pairs))
    rows = jnp.concatenate(received, axis=0)
    place = sources[:, None] == jnp.arange(n, dtype=jnp.int32)[None, :]
    ids_all = jnp.sum(jnp.where(place[:, :, None], rows[:, None, :], 0), axis=0).reshape(tokens)
    one_hot = (ids_all[:, None] == jnp.arange(VOCAB, dtype=jnp.int32)[None, :]).astype(jnp.bfloat16)
    start_rows = jnp.dot(one_hot, embed, preferred_element_type=jnp.float32).astype(jnp.bfloat16)

    proj_in = jnp.transpose(w_in[0], (1, 0, 2))
    proj_out = w_out[0]
    gains = gain.reshape(n, 1, channels)
    sfilt = short_filter[0].reshape(-1, 1, channels)
    groups = long_filter.shape[2]
    spread = (jnp.arange(channels)[None, :] // (channels // groups) == jnp.arange(groups)[:, None]).astype(jnp.float32)
    taps = jnp.dot(long_filter[0], spread, precision=lax.Precision.HIGHEST)
    short_cache = jnp.transpose(short_cycle[0], (0, 2, 1, 3))
    long_cache = long_cycle[0]
    cached, tails = prep(cached_len, short_cache, long_cache, taps, tokens)

    proj = jnp.zeros((BRANCHES, tokens, channels), jnp.bfloat16)
    prod = jnp.zeros((tokens, channels), jnp.bfloat16)
    result = jnp.zeros((tokens, channels), jnp.bfloat16)
    current = start_rows
    for turn in range(segments):
        turn_at = 2 * lanes + turn
        if turn == 0:
            blocks = [current] + [gather_step(current, step, 0, 0, lanes) for step in range(1, lanes)]
        else:
            blocks = [gather_step(current, step, turn - 1, turn, lanes) for step in range(lanes)]
        residual = blocks[0]
        carry = None
        for step, piece in enumerate(pieces_of(blocks, turn, lanes)):
            carry = in_chunk(table, step, piece, gains, proj_in, carry)
        mixed, proj, prod = mix(table, turn_at, width, carry, sfilt, taps, cached, tails, proj, prod)
        blocks = [mixed] + [gather_step(mixed, step, turn, turn, lanes) for step in range(1, lanes)]
        acc = None
        for step, piece in enumerate(pieces_of(blocks, turn, lanes)):
            if step + 1 < lanes:
                acc = out_chunk(table, step, piece, proj_out, acc)
            else:
                current, result = out_chunk(table, step, piece, proj_out, acc, (residual, result), turn_at)
    new_short, new_long = caches(cached_len, proj, prod, short_cache, long_cache)
    return result[None], jnp.transpose(new_short, (0, 2, 1, 3))[None], new_long[None]


def solution(mesh):
    in_specs = (
        P("seq"),
        P(),
        P(None, "seq"),
        P("segment", None),
        P("segment", None, None, "seq"),
        P("segment", None, None, "seq"),
        P("segment", None, "seq"),
        P("segment", None, "seq"),
        P("segment", None, None, None, "seq"),
        P("segment", None, None, "seq"),
    )
    out_specs = (
        P("segment", None, "seq"),
        P("segment", None, None, None, "seq"),
        P("segment", None, None, "seq"),
    )
    return jax.shard_map(local, mesh=mesh, in_specs=in_specs, out_specs=out_specs, check_vma=False)
```

```python
import functools

import jax
import jax.numpy as jnp
from jax import lax
from jax.experimental import pallas as pl
from jax.experimental.pallas import tpu as pltpu
from jax.sharding import PartitionSpec as P


VOCAB = 512
LONG = 128
REQUESTS = 2
BRANCHES = 3
TAIL = 8
LANE = 128
EPS = 1e-06
MIB = 1 << 20
KEPT_IN = 3
KEPT_OUT = 2
FETCHED = (0,)


WHOLE = pl.BlockSpec(memory_space=pltpu.VMEM)


def mate(lane, step, lanes):
    return lane ^ step if lanes & (lanes - 1) == 0 else (lane - step) % lanes


def send_to(lane, step, lanes):
    return lane ^ step if lanes & (lanes - 1) == 0 else (lane + step) % lanes


def gather_step(block, step, lanes):
    pairs = [(2 * i + c, 2 * send_to(i, step, lanes) + c) for i in range(lanes) for c in range(2)]
    return lax.ppermute(block, "seq", pairs)


def hop_step(block, step, source, target, lanes):
    n = 2 * lanes
    pairs = [
        (source * n + 2 * i + c, target * n + 2 * send_to(i, step, lanes) + c) for i in range(lanes) for c in range(2)
    ]
    return lax.ppermute(block, ("segment", "seq"), pairs)


def other_core(block, lanes):
    return lax.ppermute(block, "seq", [(i, i ^ 1) for i in range(2 * lanes)])


def fold(blocks, lanes, chunk):
    carry, waiting = None, []
    for turn, (step, block) in enumerate(blocks):
        if turn:
            block, carry = lax.optimization_barrier((block, carry))
        partner = other_core(block, lanes)
        carry = chunk([(2 * step, block)] + waiting, carry)
        waiting = [(2 * step + 1, partner)]
    return waiting, carry


def far_first(lanes):
    return [0] + list(range(lanes // 2, lanes)) + list(range(1, lanes // 2))


class Weights:
    def __init__(self, w, table, places):
        self.w, self.table, self.places, self.kept = w, table, places, {}


HBM = pl.BlockSpec(memory_space=pltpu.HBM)
SMEM = pl.BlockSpec(memory_space=pltpu.SMEM)


def product_call(body, weights, pieces, ins, outs, aliases, scratch, limit, flops):
    places, xs = zip(*pieces)
    branches, _, channels = weights.w.shape
    count = len(places)
    old = [p for p in places if p in weights.kept]
    new = [p for p in places if p in weights.places and p not in weights.kept]
    loose = [p for p in places if p not in old and p not in new]
    moved = new + loose
    n_in, n_out = len(ins), len(outs)

    def kernel(tab, *refs):
        x_refs, w, old_refs = refs[:count], refs[count], refs[count + 1 : count + 1 + len(old)]
        refs = refs[count + 1 + len(old) :]
        in_refs, out_refs, new_refs = refs[:n_in], refs[n_in : n_in + n_out], refs[n_in + n_out : n_in + n_out + len(new)]
        refs = refs[n_in + n_out + len(new) :]
        if moved:
            sem, refs = refs[-1], refs[:-1]
        if loose:
            buf, refs = refs[-1], refs[:-1]

        def home(p):
            if p in old:
                return old_refs[old.index(p)]
            return new_refs[new.index(p)] if p in new else buf.at[loose.index(p)]

        def fetch(p, b):
            rows = pl.ds(pl.multiple_of(tab[p] * channels, channels), channels)
            return pltpu.make_async_copy(w.at[b, rows], home(p).at[b], sem.at[moved.index(p), b])

        for p in places:
            if p in moved:
                for b in range(branches):
                    fetch(p, b).start()

        def weight_of(k, b):
            if places[k] in moved:
                fetch(places[k], b).wait()
            return home(places[k]).at[b]

        body(tab, places, x_refs, weight_of, in_refs, out_refs, refs)

    scratch = list(scratch)
    if loose:
        scratch.append(pltpu.VMEM((len(loose), branches, channels, channels), weights.w.dtype))
    if moved:
        scratch.append(pltpu.SemaphoreType.DMA((len(moved), branches)))
    shift = 2 + count + len(old)
    bytes_of = 2 * branches * channels * channels
    results = pl.pallas_call(
        kernel,
        in_specs=[SMEM] + [WHOLE] * count + [HBM] + [WHOLE] * (len(old) + n_in),
        out_specs=[WHOLE] * (n_out + len(new)),
        out_shape=list(outs) + [pltpu.VMEM((branches, channels, channels), weights.w.dtype) for _ in new],
        scratch_shapes=scratch,
        input_output_aliases={shift + i: o for i, o in aliases.items()},
        cost_estimate=pl.CostEstimate(
            flops=flops + count * bytes_of * xs[0].shape[0],
            bytes_accessed=len(moved) * bytes_of + MIB,
            transcendentals=0,
        ),
        compiler_params=pltpu.CompilerParams(vmem_limit_bytes=int(limit * MIB) + len(loose) * bytes_of),
    )(weights.table, *xs, weights.w, *[weights.kept[p] for p in old], *ins)
    weights.kept.update(zip(new, results[n_out:]))
    return results[:n_out]


def fetched(weights, places):
    branches, _, channels = weights.w.shape

    def kernel(tab, w, *refs):
        sem = refs[-1]
        copies = []
        for k, place in enumerate(places):
            rows = pl.ds(pl.multiple_of(tab[place] * channels, channels), channels)
            for b in range(branches):
                copies.append(pltpu.make_async_copy(w.at[b, rows], refs[k].at[b], sem.at[k, b]))
        for copy in copies:
            copy.start()
        for copy in copies:
            copy.wait()

    results = pl.pallas_call(
        kernel,
        in_specs=[SMEM, HBM],
        out_specs=[WHOLE] * len(places),
        out_shape=[pltpu.VMEM((branches, channels, channels), weights.w.dtype) for _ in places],
        scratch_shapes=[pltpu.SemaphoreType.DMA((len(places), branches))],
        cost_estimate=pl.CostEstimate(
            flops=0, bytes_accessed=2 * len(places) * branches * channels * channels, transcendentals=0
        ),
        compiler_params=pltpu.CompilerParams(vmem_limit_bytes=MIB, has_side_effects=True),
    )(weights.table, weights.w)
    return dict(zip(places, results))


def gained(x_ref, gain_ref, place, tab):
    wide = x_ref[...].astype(jnp.float32)
    square = wide * wide
    total = square[:, :LANE]
    for i in range(1, square.shape[1] // LANE):
        total = total + square[:, i * LANE : (i + 1) * LANE]
    return (wide * gain_ref[tab[place]]).astype(jnp.bfloat16), total


def add_products(xs, weight_of, acc_in, acc, branches):
    for k, x in enumerate(xs):
        channels = x.shape[1]
        block = min(512, channels)
        for b in range(branches):
            weights = weight_of(k, b)
            for i in range(channels // block):
                cols = pl.ds(i * block, block)
                part = jnp.dot(x, weights[:, cols], preferred_element_type=jnp.float32)
                if k:
                    acc[b, :, cols] += part
                else:
                    acc[b, :, cols] = part if acc_in is None else acc_in[b, :, cols] + part


def in_body(first, tab, places, x_refs, weight_of, in_refs, out_refs, scratch):
    gain_ref = in_refs[0]
    acc_in, total = (None, None) if first else (in_refs[1], in_refs[2][...])
    acc, ssq = out_refs
    xs = []
    for x_ref, place in zip(x_refs, places):
        x, square = gained(x_ref, gain_ref, place, tab)
        xs.append(x)
        total = square if total is None else total + square
    ssq[...] = total
    add_products(xs, weight_of, acc_in, acc, BRANCHES)


def in_chunk(weights, gain, pieces, carry):
    tokens, channels = pieces[0][1].shape
    first = carry is None
    return product_call(
        functools.partial(in_body, first),
        weights,
        pieces,
        [gain] + ([] if first else list(carry)),
        [
            jax.ShapeDtypeStruct((BRANCHES, tokens, channels), jnp.float32),
            jax.ShapeDtypeStruct((tokens, LANE), jnp.float32),
        ],
        {} if first else {1: 0, 2: 1},
        [],
        2.5,
        0,
    )


def mix_body(width, turn_at, tab, places, x_refs, weight_of, in_refs, out_refs, scratch):
    gain_ref, acc_in, ssq_in, sfilt, taps, cached, tails = in_refs[:7]
    mine = tab[turn_at] != 0
    mixed, proj, prod = out_refs
    acc, ext, f0, pz = scratch
    tokens, channels = mixed.shape
    appended = tokens // REQUESTS
    x, square = gained(x_refs[0], gain_ref, places[0], tab)
    add_products([x], weight_of, acc_in, acc, BRANCHES)
    scale = lax.rsqrt(jnp.sum(ssq_in[...] + square, axis=1, keepdims=True) / width + EPS)
    for b in range(BRANCHES):
        projected = (acc[b] * scale).astype(jnp.bfloat16)

        @pl.when(mine)
        def _(b=b, projected=projected):
            proj[b] = projected

        wide = projected.astype(jnp.float32)
        for r in range(REQUESTS):
            ext[b, r, :TAIL] = tails[r, b]
            ext[b, r, TAIL:] = wide[r * appended : (r + 1) * appended]
    pz[:, :appended] = jnp.zeros((REQUESTS, appended, channels), jnp.float32)
    block = min(256, channels)
    short = sfilt.shape[0] // BRANCHES
    strip = 8
    for r in range(REQUESTS):

        @pl.loop(0, channels // block)
        def _(i, r=r):
            cols = pl.ds(pl.multiple_of(i * block, block), block)
            rows = pl.ds(r * appended, appended)
            branches = []
            for b in range(BRANCHES):
                total = jnp.zeros((appended, block), jnp.float32)
                for j in range(short):
                    total = total + sfilt[j * BRANCHES + b, :, cols] * ext[b, r, pl.ds(TAIL - j, appended), cols]
                branches.append(total)
            product = (branches[1] * branches[2]).astype(jnp.bfloat16)
            pz[r, pl.ds(appended, appended), cols] = product.astype(jnp.float32)

            @pl.when(mine)
            def _():
                prod[rows, cols] = product

            f0[rows, cols] = branches[0]

        @pl.loop(0, channels // block)
        def _(i, r=r):
            cols = pl.ds(pl.multiple_of(i * block, block), block)
            reach = min(appended, LONG)
            sums = [cached[pl.ds(r * appended + at, strip), cols] for at in range(0, appended, strip)]
            for j in range(reach):
                tap = taps[pl.ds(j, 1), cols]
                for at in range(0, appended, strip):
                    if j < at + strip:
                        sums[at // strip] += tap * pz[r, pl.ds(appended + at - j, strip), cols]
            total = jnp.concatenate(sums, axis=0)
            rows = pl.ds(r * appended, appended)
            mixed[rows, cols] = (f0[rows, cols] * total).astype(jnp.bfloat16)


def mix(weights, gain, width, turn_at, pieces, carry, sfilt, taps, cached, tails, proj, prod):
    tokens, channels = pieces[0][1].shape
    appended = tokens // REQUESTS
    return product_call(
        functools.partial(mix_body, width, turn_at),
        weights,
        pieces,
        [gain, *carry, sfilt, taps, cached, tails, proj, prod],
        [
            jax.ShapeDtypeStruct((tokens, channels), jnp.bfloat16),
            jax.ShapeDtypeStruct((BRANCHES, tokens, channels), jnp.bfloat16),
            jax.ShapeDtypeStruct((tokens, channels), jnp.bfloat16),
        ],
        {7: 1, 8: 2},
        [
            pltpu.VMEM((BRANCHES, tokens, channels), jnp.float32),
            pltpu.VMEM((BRANCHES, REQUESTS, TAIL + appended, channels), jnp.float32),
            pltpu.VMEM((tokens, channels), jnp.float32),
            pltpu.VMEM((REQUESTS, 2 * appended, channels), jnp.float32),
        ],
        5,
        80 * tokens * channels,
    )


def out_body(first, last, turn_at, tab, places, x_refs, weight_of, in_refs, out_refs, scratch):
    acc_in = None if first else in_refs[0]
    acc = scratch[0] if last else out_refs[0]
    add_products([ref[...] for ref in x_refs], weight_of, acc_in, acc, 1)
    if last:
        rows = (in_refs[1][...].astype(jnp.float32) + acc[0]).astype(jnp.bfloat16)
        if turn_at is not None:
            rows = jnp.where(tab[turn_at] != 0, rows, in_refs[2][...])
        out_refs[0][...] = rows


def out_chunk(weights, pieces, acc, last=None, turn_at=None):
    tokens, channels = pieces[0][1].shape
    first = acc is None
    wide = jax.ShapeDtypeStruct((1, tokens, channels), jnp.float32)
    slim = jax.ShapeDtypeStruct((tokens, channels), jnp.bfloat16)
    return product_call(
        functools.partial(out_body, first, last is not None, turn_at),
        weights,
        pieces,
        ([] if first else [acc]) + ([] if last is None else list(last)),
        [wide] if last is None else [slim],
        {0: 0} if last is None and not first else {},
        [] if last is None else [pltpu.VMEM((1, tokens, channels), jnp.float32)],
        2.5,
        0,
    )[0]


def prep_kernel(lens, short, long, taps, cached, tails, ring):
    tokens, channels = cached.shape
    appended = tokens // REQUESTS
    block = min(256, channels)
    ring[LONG:] = jnp.zeros((appended, block), jnp.float32)
    for r in range(REQUESTS):
        start = lax.rem(LONG - lax.rem(lens[r], LONG), LONG)

        @pl.loop(0, channels // block)
        def _(i, r=r, start=start):
            cols = pl.ds(pl.multiple_of(i * block, block), block)
            for b in range(BRANCHES):
                tails[r, b, :, cols] = pltpu.roll(short[r, b, :, cols].astype(jnp.float32), start, 0)[LONG - TAIL :]
            ring[:LONG] = pltpu.roll(long[r, :, cols].astype(jnp.float32), start, 0)
            total = jnp.zeros((appended, block), jnp.float32)
            for j in range(1, LONG):
                total = total + taps[pl.ds(j, 1), cols] * ring[pl.ds(LONG - j, appended), :]
            cached[pl.ds(r * appended, appended), cols] = total


def prep(lens, short, long, taps, tokens):
    channels = long.shape[-1]
    appended = tokens // REQUESTS
    return pl.pallas_call(
        prep_kernel,
        in_specs=[pl.BlockSpec(memory_space=pltpu.SMEM), WHOLE, WHOLE, WHOLE],
        out_specs=[WHOLE, WHOLE],
        out_shape=[
            jax.ShapeDtypeStruct((tokens, channels), jnp.float32),
            jax.ShapeDtypeStruct((REQUESTS, BRANCHES, TAIL, channels), jnp.float32),
        ],
        scratch_shapes=[pltpu.VMEM((LONG + appended, min(256, channels)), jnp.float32)],
        cost_estimate=pl.CostEstimate(flops=256 * tokens * channels, bytes_accessed=20 * LONG * channels, transcendentals=0),
        compiler_params=pltpu.CompilerParams(vmem_limit_bytes=10 * MIB),
        name="prep",
    )(lens, short, long, taps)


def caches_kernel(lens, proj, prod, short, long, new_short, new_long, ring):
    tokens, channels = prod.shape
    appended = tokens // REQUESTS
    block = ring.shape[1]
    slots = lax.broadcasted_iota(jnp.int32, (LONG, block), 0)
    ring[...] = jnp.zeros((LONG, block), jnp.float32)
    for r in range(REQUESTS):
        at = lax.rem(lens[r], LONG)
        fresh = lax.rem(slots - at + LONG, LONG) < appended

        @pl.loop(0, channels // block)
        def _(i, r=r, at=at, fresh=fresh):
            cols = pl.ds(pl.multiple_of(i * block, block), block)
            rows = pl.ds(r * appended, appended)

            def replace(new, old):
                ring[:appended] = new.astype(jnp.float32)
                turned = pltpu.roll(ring[...], at, 0)
                return jnp.where(fresh, turned, old.astype(jnp.float32)).astype(jnp.bfloat16)

            for b in range(BRANCHES):
                new_short[r, b, :, cols] = replace(proj[b, rows, cols], short[r, b, :, cols])
            new_long[r, :, cols] = replace(prod[rows, cols], long[r, :, cols])


def caches(lens, proj, prod, short, long):
    channels = long.shape[-1]
    return pl.pallas_call(
        caches_kernel,
        in_specs=[SMEM] + [WHOLE] * 4,
        out_specs=[WHOLE, WHOLE],
        out_shape=[
            jax.ShapeDtypeStruct(short.shape, jnp.bfloat16),
            jax.ShapeDtypeStruct(long.shape, jnp.bfloat16),
        ],
        scratch_shapes=[pltpu.VMEM((LONG, min(256, channels)), jnp.float32)],
        cost_estimate=pl.CostEstimate(
            flops=8 * LONG * channels, bytes_accessed=32 * LONG * channels, transcendentals=0
        ),
        compiler_params=pltpu.CompilerParams(vmem_limit_bytes=6 * MIB),
        name="caches",
    )(lens, proj, prod, short, long)


def local(
    token_ids,
    cached_len,
    embed,
    gain,
    w_in,
    short_filter,
    long_filter,
    w_out,
    short_cycle,
    long_cycle,
):
    segments = lax.axis_size("segment")
    n = lax.axis_size("seq")
    lanes = n // 2
    own_tokens = token_ids.shape[0]
    tokens = own_tokens * n
    channels = embed.shape[1]
    width = gain.shape[1]
    my_segment = lax.axis_index("segment")
    me = lax.axis_index("seq")
    lane, core = me // 2, me % 2

    steps = jnp.arange(2 * lanes, dtype=jnp.int32)
    sources = 2 * mate(lane, steps // 2, lanes) + (core ^ (steps % 2))
    mine = (jnp.arange(segments, dtype=jnp.int32) == my_segment).astype(jnp.int32)
    table = jnp.concatenate([sources.astype(jnp.int32), mine])

    pair = jnp.stack([token_ids, other_core(token_ids, lanes)])
    received = [pair]
    for step in range(1, lanes):
        received.append(gather_step(pair, step, lanes))
    rows = jnp.concatenate(received, axis=0)
    place = sources[:, None] == jnp.arange(n, dtype=jnp.int32)[None, :]
    ids_all = jnp.sum(jnp.where(place[:, :, None], rows[:, None, :], 0), axis=0).reshape(tokens)
    one_hot = (ids_all[:, None] == jnp.arange(VOCAB, dtype=jnp.int32)[None, :]).astype(jnp.bfloat16)
    start_rows = jnp.dot(one_hot, embed, preferred_element_type=jnp.float32).astype(jnp.bfloat16)

    def held(order, rounds):
        return {2 * step + half for step in order[max(0, lanes - rounds) :] for half in range(2)}

    def in_hbm(w):
        return pltpu.with_memory_space_constraint(w, pltpu.HBM)

    proj_in = Weights(in_hbm(jnp.transpose(w_in[0], (1, 0, 2))), table, held(list(range(lanes)), KEPT_IN))
    proj_out = Weights(in_hbm(w_out), table, held(far_first(lanes), KEPT_OUT))
    gains = gain.reshape(n, 1, channels)
    sfilt = short_filter[0].reshape(-1, 1, channels)
    groups = long_filter.shape[2]
    spread = (jnp.arange(channels)[None, :] // (channels // groups) == jnp.arange(groups)[:, None]).astype(jnp.float32)
    taps = jnp.dot(long_filter[0], spread, precision=lax.Precision.HIGHEST)
    short_cache = jnp.transpose(short_cycle[0], (0, 2, 1, 3))
    long_cache = long_cycle[0]
    cached, tails = prep(cached_len, short_cache, long_cache, taps, tokens)

    proj = jnp.zeros((BRANCHES, tokens, channels), jnp.bfloat16)
    prod = jnp.zeros((tokens, channels), jnp.bfloat16)
    result = jnp.zeros((tokens, channels), jnp.bfloat16)
    current = start_rows
    for turn in range(segments):
        turn_at = 2 * lanes + turn
        blocks = [(0, current)] if turn == 0 else []
        for step in range(len(blocks), lanes):
            if turn == 0:
                blocks.append((step, gather_step(current, step, lanes)))
            else:
                blocks.append((step, hop_step(current, step, turn - 1, turn, lanes)))
        residual = blocks[0][1]
        fetch = [place for place in FETCHED if place not in proj_in.places]
        if turn and fetch:
            proj_in.kept.update(fetched(proj_in, fetch))
        waiting, carry = fold(blocks, lanes, functools.partial(in_chunk, proj_in, gains))
        mixed, proj, prod = mix(proj_in, gains, width, turn_at, waiting, carry, sfilt, taps, cached, tails, proj, prod)
        blocks = [(0, mixed)]
        for step in far_first(lanes)[1:]:
            blocks.append((step, gather_step(mixed, step, lanes)))
        waiting, acc = fold(blocks, lanes, functools.partial(out_chunk, proj_out))
        if turn + 1 < segments:
            current = out_chunk(proj_out, waiting, acc, (residual,))
            result = jnp.where(my_segment == turn, current, result)
        else:
            new_short, new_long = caches(cached_len, proj, prod, short_cache, long_cache)
            result = out_chunk(proj_out, waiting, acc, (residual, result), turn_at)
    return result[None], jnp.transpose(new_short, (0, 2, 1, 3))[None], new_long[None]


def solution(mesh):
    in_specs = (
        P("seq"),
        P(),
        P(None, "seq"),
        P("segment", None),
        P("segment", None, None, "seq"),
        P("segment", None, None, "seq"),
        P("segment", None, "seq"),
        P("segment", None, "seq"),
        P("segment", None, None, None, "seq"),
        P("segment", None, None, "seq"),
    )
    out_specs = (
        P("segment", None, "seq"),
        P("segment", None, None, None, "seq"),
        P("segment", None, None, "seq"),
    )
    return jax.shard_map(local, mesh=mesh, in_specs=in_specs, out_specs=out_specs, check_vma=False)
```

```python
import functools

import jax
import jax.numpy as jnp
from jax import lax
from jax.experimental import pallas as pl
from jax.experimental.pallas import tpu as pltpu
from jax.sharding import PartitionSpec as P


VOCAB = 512
LONG = 128
REQUESTS = 2
BRANCHES = 3
TAIL = 8
STRIP = 8
LANE = 128
EPS = 1e-06
MIB = 1 << 20
KEPT_IN = 3
KEPT_OUT = 2
FETCHED = (0,)


WHOLE = pl.BlockSpec(memory_space=pltpu.VMEM)


def mate(lane, step, lanes):
    return lane ^ step if lanes & (lanes - 1) == 0 else (lane - step) % lanes


def send_to(lane, step, lanes):
    return lane ^ step if lanes & (lanes - 1) == 0 else (lane + step) % lanes


def gather_step(block, step, lanes):
    pairs = [(2 * i + c, 2 * send_to(i, step, lanes) + c) for i in range(lanes) for c in range(2)]
    return lax.ppermute(block, "seq", pairs)


def hop_step(block, step, source, target, lanes):
    n = 2 * lanes
    pairs = [
        (source * n + 2 * i + c, target * n + 2 * send_to(i, step, lanes) + c) for i in range(lanes) for c in range(2)
    ]
    return lax.ppermute(block, ("segment", "seq"), pairs)


def other_core(block, lanes):
    return lax.ppermute(block, "seq", [(i, i ^ 1) for i in range(2 * lanes)])


def fold(blocks, lanes, chunk, plan):
    carry, waiting, count = None, [], 0
    for turn, group in enumerate(plan):
        after = plan[turn + 1] if turn + 1 < len(plan) else []
        ahead = [2 * step for step in after] + [2 * step + 1 for step in group]
        if not group:
            carry = chunk(waiting, carry, ahead)
            waiting = []
            continue
        group = [(step, blocks[step]) for step in group]
        if turn:
            arrived, carry = lax.optimization_barrier(([block for _, block in group], carry))
            group = [(step, block) for (step, _), block in zip(group, arrived)]
        partners = []
        for step, block in group:
            partners.append((2 * step + 1, other_core(block, lanes)))
            count += 1
        carry = chunk([(2 * step, block) for step, block in group] + waiting, carry, ahead)
        waiting = partners
    return waiting, carry


def one_by_one(lanes):
    return [[step] for step in range(lanes)]


def near_then_rest(lanes):
    plan = one_by_one(lanes)
    return plan if lanes < 3 else plan[:-2] + [[], [lanes - 2, lanes - 1]]


def far_then_near(lanes):
    if lanes < 4:
        return one_by_one(lanes)
    half = lanes // 2
    far = [list(range(step, min(step + 2, lanes))) for step in range(half, lanes, 2)]
    return [[0], []] + far + [[step] for step in range(1, half)]


class Weights:
    def __init__(self, w, table, places):
        self.w, self.table, self.places, self.kept = w, table, places, {}
        self.lanes = w.shape[1] // (2 * w.shape[2])


HBM = pl.BlockSpec(memory_space=pltpu.HBM)
SMEM = pl.BlockSpec(memory_space=pltpu.SMEM)


def product_call(body, weights, pieces, ins, outs, aliases, scratch, limit, flops, extra=()):
    places, xs = zip(*pieces)
    branches, _, channels = weights.w.shape
    count = len(places)
    old = [p for p in places if p in weights.kept]
    extra = [p for p in extra if p not in weights.kept]
    new = [p for p in places if p in weights.places and p not in weights.kept] + extra
    loose = [p for p in places if p not in old and p not in new]
    moved = new + loose
    n_in, n_out = len(ins), len(outs)

    def kernel(tab, *refs):
        x_refs, w, old_refs = refs[:count], refs[count], refs[count + 1 : count + 1 + len(old)]
        refs = refs[count + 1 + len(old) :]
        in_refs, out_refs, new_refs = refs[:n_in], refs[n_in : n_in + n_out], refs[n_in + n_out : n_in + n_out + len(new)]
        refs = refs[n_in + n_out + len(new) :]
        if moved:
            sem, refs = refs[-1], refs[:-1]
        if loose:
            buf, refs = refs[-1], refs[:-1]

        def home(p):
            if p in old:
                return old_refs[old.index(p)]
            return new_refs[new.index(p)] if p in new else buf.at[loose.index(p)]

        def fetch(p, b):
            rows = pl.ds(pl.multiple_of(tab[p] * channels, channels), channels)
            return pltpu.make_async_copy(w.at[b, rows], home(p).at[b], sem.at[moved.index(p), b])

        for b in range(branches):
            for p in [*places, *extra]:
                if p in moved:
                    fetch(p, b).start()

        def weight_of(k, b):
            if places[k] in moved:
                fetch(places[k], b).wait()
            return home(places[k]).at[b]

        body(tab, places, x_refs, weight_of, in_refs, out_refs, refs)
        for p in extra:
            for b in range(branches):
                fetch(p, b).wait()

    scratch = list(scratch)
    if loose:
        scratch.append(pltpu.VMEM((len(loose), branches, channels, channels), weights.w.dtype))
    if moved:
        scratch.append(pltpu.SemaphoreType.DMA((len(moved), branches)))
    shift = 2 + count + len(old)
    bytes_of = 2 * branches * channels * channels
    results = pl.pallas_call(
        kernel,
        in_specs=[SMEM] + [WHOLE] * count + [HBM] + [WHOLE] * (len(old) + n_in),
        out_specs=[WHOLE] * (n_out + len(new)),
        out_shape=list(outs) + [pltpu.VMEM((branches, channels, channels), weights.w.dtype) for _ in new],
        scratch_shapes=scratch,
        input_output_aliases={shift + i: o for i, o in aliases.items()},
        cost_estimate=pl.CostEstimate(
            flops=flops + count * bytes_of * xs[0].shape[0],
            bytes_accessed=len(moved) * bytes_of + MIB,
            transcendentals=0,
        ),
        compiler_params=pltpu.CompilerParams(vmem_limit_bytes=int(limit * MIB) + len(loose) * bytes_of),
    )(weights.table, *xs, weights.w, *[weights.kept[p] for p in old], *ins)
    weights.kept.update(zip(new, results[n_out:]))
    return results[:n_out]


def fetched(weights, places):
    branches, _, channels = weights.w.shape

    def kernel(tab, w, *refs):
        sem = refs[-1]
        copies = []
        for k, place in enumerate(places):
            rows = pl.ds(pl.multiple_of(tab[place] * channels, channels), channels)
            for b in range(branches):
                copies.append(pltpu.make_async_copy(w.at[b, rows], refs[k].at[b], sem.at[k, b]))
        for copy in copies:
            copy.start()
        for copy in copies:
            copy.wait()

    results = pl.pallas_call(
        kernel,
        in_specs=[SMEM, HBM],
        out_specs=[WHOLE] * len(places),
        out_shape=[pltpu.VMEM((branches, channels, channels), weights.w.dtype) for _ in places],
        scratch_shapes=[pltpu.SemaphoreType.DMA((len(places), branches))],
        cost_estimate=pl.CostEstimate(
            flops=0, bytes_accessed=2 * len(places) * branches * channels * channels, transcendentals=0
        ),
        compiler_params=pltpu.CompilerParams(vmem_limit_bytes=MIB, has_side_effects=True),
    )(weights.table, weights.w)
    return dict(zip(places, results))


def gained(x_ref, gain_ref, place, tab):
    wide = x_ref[...].astype(jnp.float32)
    square = wide * wide
    total = square[:, :LANE]
    for i in range(1, square.shape[1] // LANE):
        total = total + square[:, i * LANE : (i + 1) * LANE]
    return (wide * gain_ref[tab[place]]).astype(jnp.bfloat16), total


def add_products(x_refs, weight_of, acc_in, acc, branches, looped):
    channels = x_refs[0].shape[-1]
    block = min(512, channels)

    def branch(b):
        weights = [weight_of(k, b) for k in range(len(x_refs))]
        for i in range(channels // block):
            cols = pl.ds(i * block, block)
            total = None if acc_in is None else acc_in[b, :, cols]
            for x, w in zip(x_refs, weights):
                part = jnp.dot(x[...], w[:, cols], preferred_element_type=jnp.float32)
                total = part if total is None else total + part
            acc[b, :, cols] = total

    if looped:
        pl.loop(0, branches)(branch)
    else:
        for b in range(branches):
            branch(b)


def in_body(first, looped, tab, places, x_refs, weight_of, in_refs, out_refs, scratch):
    gain_ref = in_refs[0]
    acc_in, total = (None, None) if first else (in_refs[1], in_refs[2][...])
    acc, ssq = out_refs
    xs = [scratch[0].at[k] for k in range(len(places))]
    for x_ref, x, place in zip(x_refs, xs, places):
        x[...], square = gained(x_ref, gain_ref, place, tab)
        total = square if total is None else total + square
    ssq[...] = total
    add_products(xs, weight_of, acc_in, acc, BRANCHES, looped)


def in_chunk(weights, gain, pieces, carry, ahead=()):
    filling = bool(weights.places - weights.kept.keys())
    tokens, channels = pieces[0][1].shape
    first = carry is None
    return product_call(
        functools.partial(in_body, first, filling),
        weights,
        pieces,
        [gain] + ([] if first else list(carry)),
        [
            jax.ShapeDtypeStruct((BRANCHES, tokens, channels), jnp.float32),
            jax.ShapeDtypeStruct((tokens, LANE), jnp.float32),
        ],
        {} if first else {1: 0, 2: 1},
        [pltpu.VMEM((len(pieces), tokens, channels), jnp.bfloat16)],
        2.5,
        0,
        ahead if filling else (),
    )


def add_taps(sums, strip_at, taps, cols, first, reach):
    count = len(sums)
    for rest in range(STRIP):
        held = {}
        for m in range(count - 1, -(LONG // STRIP) - 1, -1):
            start = STRIP * m - rest
            if first == 0 and start + STRIP <= 0 or first == 1 and (start >= 0 or start < -LONG):
                continue
            uses = [a for a in range(count) if first <= STRIP * (a - m) + rest < reach]
            if not uses:
                continue
            rows = strip_at(start)
            for a in uses:
                j = STRIP * (a - m) + rest
                if j not in held:
                    held[j] = taps[pl.ds(j, 1), cols]
                sums[a] += held[j] * rows


def mix_body(width, turn_at, looped, tab, places, x_refs, weight_of, in_refs, out_refs, scratch):
    gain_ref, acc_in, ssq_in, sfilt, taps, cached, tails = in_refs[:7]
    mine = tab[turn_at] != 0
    mixed, proj, prod = out_refs
    acc, xg, ext, pz = scratch
    tokens, channels = mixed.shape
    appended = tokens // REQUESTS
    xs = [xg.at[k] for k in range(len(places))]
    total = ssq_in[...]
    for x_ref, x, place in zip(x_refs, xs, places):
        x[...], square = gained(x_ref, gain_ref, place, tab)
        total = total + square
    add_products(xs, weight_of, acc_in, acc, BRANCHES, looped)
    scale = lax.rsqrt(jnp.sum(total, axis=1, keepdims=True) / width + EPS)
    for b in range(BRANCHES):
        projected = (acc[b] * scale).astype(jnp.bfloat16)

        @pl.when(mine)
        def _(b=b, projected=projected):
            proj[b] = projected

        wide = projected.astype(jnp.float32)
        for r in range(REQUESTS):
            ext[b, r, :TAIL] = tails[r, b]
            ext[b, r, TAIL:] = wide[r * appended : (r + 1) * appended]
    pz[:appended] = jnp.zeros((appended, channels), jnp.float32)
    block = min(256, channels)
    short = sfilt.shape[0] // BRANCHES

    @pl.loop(0, REQUESTS)
    def _(r):
        rows = pl.ds(pl.multiple_of(r * appended, appended), appended)

        @pl.loop(0, channels // block)
        def _(i):
            cols = pl.ds(pl.multiple_of(i * block, block), block)
            branches = []
            for b in range(BRANCHES):
                total = jnp.zeros((appended, block), jnp.float32)
                for j in range(short):
                    total = total + sfilt[j * BRANCHES + b, :, cols] * ext[b, r, pl.ds(TAIL - j, appended), cols]
                branches.append(total)
            product = (branches[1] * branches[2]).astype(jnp.bfloat16)
            pz[pl.ds(appended, appended), cols] = product.astype(jnp.float32)

            @pl.when(mine)
            def _():
                prod[rows, cols] = product

            sums = [cached[r, pl.ds(at, STRIP), cols] for at in range(0, appended, STRIP)]
            add_taps(sums, lambda at: pz[pl.ds(appended + at, STRIP), cols], taps, cols, 0, min(appended, LONG))
            mixed[rows, cols] = (branches[0] * jnp.concatenate(sums, axis=0)).astype(jnp.bfloat16)


def mix(weights, gain, width, turn_at, pieces, carry, sfilt, taps, cached, tails, proj, prod):
    tokens, channels = pieces[0][1].shape
    appended = tokens // REQUESTS
    return product_call(
        functools.partial(mix_body, width, turn_at, bool(weights.places - weights.kept.keys())),
        weights,
        pieces,
        [gain, *carry, sfilt, taps, cached, tails, proj, prod],
        [
            jax.ShapeDtypeStruct((tokens, channels), jnp.bfloat16),
            jax.ShapeDtypeStruct((BRANCHES, tokens, channels), jnp.bfloat16),
            jax.ShapeDtypeStruct((tokens, channels), jnp.bfloat16),
        ],
        {7: 1, 8: 2},
        [
            pltpu.VMEM((BRANCHES, tokens, channels), jnp.float32),
            pltpu.VMEM((len(pieces), tokens, channels), jnp.bfloat16),
            pltpu.VMEM((BRANCHES, REQUESTS, TAIL + appended, channels), jnp.float32),
            pltpu.VMEM((2 * appended, channels), jnp.float32),
        ],
        5,
        80 * tokens * channels,
    )


def out_body(first, last, turn_at, tab, places, x_refs, weight_of, in_refs, out_refs, scratch):
    acc_in = None if first else in_refs[0]
    acc = scratch[0] if last else out_refs[0]
    add_products(x_refs, weight_of, acc_in, acc, 1, False)
    if last:
        rows = (in_refs[1][...].astype(jnp.float32) + acc[0]).astype(jnp.bfloat16)
        for turn, earlier in enumerate(in_refs[2:]):
            rows = jnp.where(tab[turn_at + turn] != 0, earlier[...], rows)
        out_refs[0][...] = rows


def out_chunk(weights, pieces, acc, ahead=(), last=None, turn_at=None):
    extra = ()
    if acc is None:
        for p in [p for p in weights.kept if p not in weights.places]:
            weights.kept.pop(p)
        extra = [p for p in range(2 * weights.lanes) if p not in weights.kept and p != pieces[0][0]]
    tokens, channels = pieces[0][1].shape
    first = acc is None
    wide = jax.ShapeDtypeStruct((1, tokens, channels), jnp.float32)
    slim = jax.ShapeDtypeStruct((tokens, channels), jnp.bfloat16)
    return product_call(
        functools.partial(out_body, first, last is not None, turn_at),
        weights,
        pieces,
        ([] if first else [acc]) + ([] if last is None else list(last)),
        [wide] if last is None else [slim],
        {0: 0} if last is None and not first else {},
        [] if last is None else [pltpu.VMEM((1, tokens, channels), jnp.float32)],
        2.5,
        0,
        extra,
    )[0]


def prep_kernel(lens, short_hbm, long_hbm, taps, cached, tails, short, long, ring, sem):
    copies = [
        pltpu.make_async_copy(long_hbm, long, sem.at[0]),
        pltpu.make_async_copy(short_hbm, short, sem.at[1]),
    ]
    for copy in copies:
        copy.start()
    for copy in copies:
        copy.wait()
    appended, channels = cached.shape[1:]
    block = min(256, channels)
    ring[LONG:] = jnp.zeros((STRIP, block), jnp.float32)

    @pl.loop(0, REQUESTS)
    def _(r):
        rows = lax.broadcasted_iota(jnp.int32, (LONG, LONG), 0) + lax.rem(lens[r], LONG)
        turn = (lax.rem(rows, LONG) == lax.broadcasted_iota(jnp.int32, (LONG, LONG), 1)).astype(jnp.bfloat16)

        @pl.loop(0, channels // block)
        def _(i):
            cols = pl.ds(pl.multiple_of(i * block, block), block)
            for b in range(BRANCHES):
                newest = jnp.dot(turn[LONG - 2 * TAIL :], short[r, b, :, cols], preferred_element_type=jnp.float32)
                tails[r, b, :, cols] = newest[TAIL:]
            ring[:LONG] = jnp.dot(turn, long[r, :, cols], preferred_element_type=jnp.float32)
            sums = [jnp.zeros((STRIP, block), jnp.float32) for _ in range(0, appended, STRIP)]
            add_taps(sums, lambda at: ring[pl.ds(LONG + at, STRIP), :], taps, cols, 1, LONG)
            cached[r, :, cols] = jnp.concatenate(sums, axis=0)


def prep(lens, short, long, taps, tokens):
    channels = long.shape[-1]
    appended = tokens // REQUESTS
    return pl.pallas_call(
        prep_kernel,
        in_specs=[SMEM, HBM, HBM, WHOLE],
        out_specs=[WHOLE, WHOLE],
        out_shape=[
            jax.ShapeDtypeStruct((REQUESTS, appended, channels), jnp.float32),
            jax.ShapeDtypeStruct((REQUESTS, BRANCHES, TAIL, channels), jnp.float32),
        ],
        scratch_shapes=[
            pltpu.VMEM(short.shape, short.dtype),
            pltpu.VMEM(long.shape, long.dtype),
            pltpu.VMEM((LONG + STRIP, min(256, channels)), jnp.float32),
            pltpu.SemaphoreType.DMA((2,)),
        ],
        cost_estimate=pl.CostEstimate(flops=256 * tokens * channels, bytes_accessed=20 * LONG * channels, transcendentals=0),
        compiler_params=pltpu.CompilerParams(vmem_limit_bytes=8 * MIB),
        name="prep",
    )(lens, short, long, taps)


def caches_kernel(lens, proj, prod, short, long, new_short, new_long):
    tokens, channels = prod.shape
    appended = tokens // REQUESTS
    block = min(256, channels)
    slots = lax.broadcasted_iota(jnp.int32, (LONG, block), 0)

    @pl.loop(0, REQUESTS)
    def _(r):
        at = lax.rem(lens[r], LONG)
        fresh = lax.rem(slots - at + LONG, LONG) < appended
        token = lax.rem(lax.broadcasted_iota(jnp.int32, (LONG, appended), 0) - at + LONG, LONG)
        place = (token == lax.broadcasted_iota(jnp.int32, (LONG, appended), 1)).astype(jnp.bfloat16)
        rows = pl.ds(pl.multiple_of(r * appended, appended), appended)

        @pl.loop(0, channels // block)
        def _(i):
            cols = pl.ds(pl.multiple_of(i * block, block), block)

            def replace(new, old):
                turned = jnp.dot(place, new, preferred_element_type=jnp.float32)
                return jnp.where(fresh, turned, old.astype(jnp.float32)).astype(jnp.bfloat16)

            for b in range(BRANCHES):
                new_short[r, b, :, cols] = replace(proj[b, rows, cols], short[r, b, :, cols])
            new_long[r, :, cols] = replace(prod[rows, cols], long[r, :, cols])


def caches(lens, proj, prod, short, long):
    channels = long.shape[-1]
    return pl.pallas_call(
        caches_kernel,
        in_specs=[SMEM] + [WHOLE] * 4,
        out_specs=[WHOLE, WHOLE],
        out_shape=[
            jax.ShapeDtypeStruct(short.shape, jnp.bfloat16),
            jax.ShapeDtypeStruct(long.shape, jnp.bfloat16),
        ],
        cost_estimate=pl.CostEstimate(
            flops=8 * LONG * channels, bytes_accessed=32 * LONG * channels, transcendentals=0
        ),
        compiler_params=pltpu.CompilerParams(vmem_limit_bytes=6 * MIB),
        name="caches",
    )(lens, proj, prod, short, long)


def local(
    token_ids,
    cached_len,
    embed,
    gain,
    w_in,
    short_filter,
    long_filter,
    w_out,
    short_cycle,
    long_cycle,
):
    def in_hbm(w):
        return pltpu.with_memory_space_constraint(w, pltpu.HBM)

    segments = lax.axis_size("segment")
    n = lax.axis_size("seq")
    lanes = n // 2
    own_tokens = token_ids.shape[0]
    tokens = own_tokens * n
    channels = embed.shape[1]
    width = gain.shape[1]
    my_segment = lax.axis_index("segment")
    me = lax.axis_index("seq")
    lane, core = me // 2, me % 2

    steps = jnp.arange(2 * lanes, dtype=jnp.int32)
    sources = 2 * mate(lane, steps // 2, lanes) + (core ^ (steps % 2))
    mine = (jnp.arange(segments, dtype=jnp.int32) == my_segment).astype(jnp.int32)
    table = jnp.concatenate([sources.astype(jnp.int32), mine])

    pair = jnp.stack([token_ids, other_core(token_ids, lanes)])
    received = [pair]
    for step in range(1, lanes):
        received.append(gather_step(pair, step, lanes))
    rows = jnp.concatenate(received, axis=0)
    place = sources[:, None] == jnp.arange(n, dtype=jnp.int32)[None, :]
    ids_all = jnp.sum(jnp.where(place[:, :, None], rows[:, None, :], 0), axis=0).reshape(tokens)
    one_hot = (ids_all[:, None] == jnp.arange(VOCAB, dtype=jnp.int32)[None, :]).astype(jnp.bfloat16)
    start_rows = jnp.dot(one_hot, embed, preferred_element_type=jnp.float32).astype(jnp.bfloat16)

    def held(order, rounds):
        return {2 * step + half for step in order[max(0, lanes - rounds) :] for half in range(2)}

    proj_in = Weights(in_hbm(jnp.transpose(w_in[0], (1, 0, 2))), table, held(list(range(lanes)), KEPT_IN))
    proj_out = Weights(in_hbm(w_out), table, held(list(range(lanes)), KEPT_OUT))
    gains = gain.reshape(n, 1, channels)
    sfilt = short_filter[0].reshape(-1, 1, channels)
    groups = long_filter.shape[2]
    spread = (jnp.arange(channels)[None, :] // (channels // groups) == jnp.arange(groups)[:, None]).astype(jnp.float32)
    taps = jnp.dot(long_filter[0], spread, precision=lax.Precision.HIGHEST)
    short_cache = jnp.transpose(short_cycle[0], (0, 2, 1, 3))
    long_cache = long_cycle[0]
    cached, tails = prep(cached_len, in_hbm(short_cache), in_hbm(long_cache), taps, tokens)

    proj = jnp.zeros((BRANCHES, tokens, channels), jnp.bfloat16)
    prod = jnp.zeros((tokens, channels), jnp.bfloat16)
    results = []
    current = start_rows
    for turn in range(segments):
        turn_at = 2 * lanes + turn
        blocks = {0: current} if turn == 0 else {}
        for step in range(len(blocks), lanes):
            if turn == 0:
                blocks[step] = gather_step(current, step, lanes)
            else:
                blocks[step] = hop_step(current, step, turn - 1, turn, lanes)
        residual = blocks[0]
        fetch = [place for place in FETCHED if place not in proj_in.places]
        if turn == 1:
            proj_in.kept.pop(1, None)
        if turn and fetch:
            proj_in.kept.update(fetched(proj_in, fetch))
        plan = far_then_near(lanes) if turn else one_by_one(lanes)
        waiting, carry = fold(blocks, lanes, functools.partial(in_chunk, proj_in, gains), plan)
        mixed, proj, prod = mix(proj_in, gains, width, turn_at, waiting, carry, sfilt, taps, cached, tails, proj, prod)
        blocks = {0: mixed}
        for step in range(1, lanes):
            blocks[step] = gather_step(mixed, step, lanes)
        waiting, acc = fold(blocks, lanes, functools.partial(out_chunk, proj_out), near_then_rest(lanes))
        if turn + 1 < segments:
            current = out_chunk(proj_out, waiting, acc, last=(residual,))
            results.append(current)
        else:
            new_short, new_long = caches(cached_len, proj, prod, short_cache, long_cache)
            result = out_chunk(proj_out, waiting, acc, last=(residual, *results), turn_at=2 * lanes)
    return result[None], jnp.transpose(new_short, (0, 2, 1, 3))[None], new_long[None]


def solution(mesh):
    in_specs = (
        P("seq"),
        P(),
        P(None, "seq"),
        P("segment", None),
        P("segment", None, None, "seq"),
        P("segment", None, None, "seq"),
        P("segment", None, "seq"),
        P("segment", None, "seq"),
        P("segment", None, None, None, "seq"),
        P("segment", None, None, "seq"),
    )
    out_specs = (
        P("segment", None, "seq"),
        P("segment", None, None, None, "seq"),
        P("segment", None, None, "seq"),
    )
    return jax.shard_map(local, mesh=mesh, in_specs=in_specs, out_specs=out_specs, check_vma=False)
```

```python
import functools

import jax
import jax.numpy as jnp
from jax import lax
from jax.experimental import pallas as pl
from jax.experimental.pallas import tpu as pltpu
from jax.sharding import PartitionSpec as P


VOCAB = 512
LONG = 128
REQUESTS = 2
BRANCHES = 3
TAIL = 8
STRIP = 8
LANE = 128
EPS = 1e-06
MIB = 1 << 20
KEPT_IN = 3
KEPT_OUT = 2
FETCHED = (0,)


WHOLE = pl.BlockSpec(memory_space=pltpu.VMEM)


def mate(lane, step, lanes):
    return lane ^ step if lanes & (lanes - 1) == 0 else (lane - step) % lanes


def send_to(lane, step, lanes):
    return lane ^ step if lanes & (lanes - 1) == 0 else (lane + step) % lanes


def gather_step(block, step, lanes):
    pairs = [(2 * i + c, 2 * send_to(i, step, lanes) + c) for i in range(lanes) for c in range(2)]
    return lax.ppermute(block, "seq", pairs)


def hop_step(block, step, source, target, lanes):
    n = 2 * lanes
    pairs = [
        (source * n + 2 * i + c, target * n + 2 * send_to(i, step, lanes) + c) for i in range(lanes) for c in range(2)
    ]
    return lax.ppermute(block, ("segment", "seq"), pairs)


def other_core(block, lanes):
    return lax.ppermute(block, "seq", [(i, i ^ 1) for i in range(2 * lanes)])


def fold(blocks, lanes, chunk, plan):
    carry, waiting, count = None, [], 0
    for turn, group in enumerate(plan):
        after = plan[turn + 1] if turn + 1 < len(plan) else []
        ahead = [2 * step for step in after] + [2 * step + 1 for step in group]
        if not group:
            carry = chunk(waiting, carry, ahead)
            waiting = []
            continue
        group = [(step, blocks[step]) for step in group]
        if turn:
            arrived, carry = lax.optimization_barrier(([block for _, block in group], carry))
            group = [(step, block) for (step, _), block in zip(group, arrived)]
        partners = []
        for step, block in group:
            partners.append((2 * step + 1, other_core(block, lanes)))
            count += 1
        carry = chunk([(2 * step, block) for step, block in group] + waiting, carry, ahead)
        waiting = partners
    return waiting, carry


def one_by_one(lanes):
    return [[step] for step in range(lanes)]


def near_then_rest(lanes):
    plan = one_by_one(lanes)
    return plan if lanes < 3 else plan[:-2] + [[], [lanes - 2, lanes - 1]]


def far_then_near(lanes):
    if lanes < 4:
        return one_by_one(lanes)
    half = lanes // 2
    far = [list(range(step, min(step + 2, lanes))) for step in range(half, lanes, 2)]
    return [[0], []] + far + [[step] for step in range(1, half)]


class Weights:
    def __init__(self, w, table, places):
        self.w, self.table, self.places, self.kept = w, table, places, {}
        self.lanes = w.shape[1] // (2 * w.shape[2])


HBM = pl.BlockSpec(memory_space=pltpu.HBM)
SMEM = pl.BlockSpec(memory_space=pltpu.SMEM)


def product_call(body, weights, pieces, ins, outs, aliases, scratch, limit, flops, extra=()):
    places, xs = zip(*pieces)
    branches, _, channels = weights.w.shape
    count = len(places)
    old = [p for p in places if p in weights.kept]
    extra = [p for p in extra if p not in weights.kept]
    new = [p for p in places if p in weights.places and p not in weights.kept] + extra
    loose = [p for p in places if p not in old and p not in new]
    moved = new + loose
    n_in, n_out = len(ins), len(outs)

    def kernel(tab, *refs):
        x_refs, w, old_refs = refs[:count], refs[count], refs[count + 1 : count + 1 + len(old)]
        refs = refs[count + 1 + len(old) :]
        in_refs, out_refs, new_refs = refs[:n_in], refs[n_in : n_in + n_out], refs[n_in + n_out : n_in + n_out + len(new)]
        refs = refs[n_in + n_out + len(new) :]
        if moved:
            sem, refs = refs[-1], refs[:-1]
        if loose:
            buf, refs = refs[-1], refs[:-1]

        def home(p):
            if p in old:
                return old_refs[old.index(p)]
            return new_refs[new.index(p)] if p in new else buf.at[loose.index(p)]

        def fetch(p, b):
            rows = pl.ds(pl.multiple_of(tab[p] * channels, channels), channels)
            return pltpu.make_async_copy(w.at[b, rows], home(p).at[b], sem.at[moved.index(p), b])

        for b in range(branches):
            for p in [*places, *extra]:
                if p in moved:
                    fetch(p, b).start()

        def weight_of(k, b):
            if places[k] in moved:
                fetch(places[k], b).wait()
            return home(places[k]).at[b]

        body(tab, places, x_refs, weight_of, in_refs, out_refs, refs)
        for p in extra:
            for b in range(branches):
                fetch(p, b).wait()

    scratch = list(scratch)
    if loose:
        scratch.append(pltpu.VMEM((len(loose), branches, channels, channels), weights.w.dtype))
    if moved:
        scratch.append(pltpu.SemaphoreType.DMA((len(moved), branches)))
    shift = 2 + count + len(old)
    bytes_of = 2 * branches * channels * channels
    results = pl.pallas_call(
        kernel,
        in_specs=[SMEM] + [WHOLE] * count + [HBM] + [WHOLE] * (len(old) + n_in),
        out_specs=[WHOLE] * (n_out + len(new)),
        out_shape=list(outs) + [pltpu.VMEM((branches, channels, channels), weights.w.dtype) for _ in new],
        scratch_shapes=scratch,
        input_output_aliases={shift + i: o for i, o in aliases.items()},
        cost_estimate=pl.CostEstimate(
            flops=flops + count * bytes_of * xs[0].shape[0],
            bytes_accessed=len(moved) * bytes_of + MIB,
            transcendentals=0,
        ),
        compiler_params=pltpu.CompilerParams(vmem_limit_bytes=int(limit * MIB) + len(loose) * bytes_of),
    )(weights.table, *xs, weights.w, *[weights.kept[p] for p in old], *ins)
    weights.kept.update(zip(new, results[n_out:]))
    return results[:n_out]


def fetched(weights, places):
    branches, _, channels = weights.w.shape

    def kernel(tab, w, *refs):
        sem = refs[-1]
        copies = []
        for k, place in enumerate(places):
            rows = pl.ds(pl.multiple_of(tab[place] * channels, channels), channels)
            for b in range(branches):
                copies.append(pltpu.make_async_copy(w.at[b, rows], refs[k].at[b], sem.at[k, b]))
        for copy in copies:
            copy.start()
        for copy in copies:
            copy.wait()

    results = pl.pallas_call(
        kernel,
        in_specs=[SMEM, HBM],
        out_specs=[WHOLE] * len(places),
        out_shape=[pltpu.VMEM((branches, channels, channels), weights.w.dtype) for _ in places],
        scratch_shapes=[pltpu.SemaphoreType.DMA((len(places), branches))],
        cost_estimate=pl.CostEstimate(
            flops=0, bytes_accessed=2 * len(places) * branches * channels * channels, transcendentals=0
        ),
        compiler_params=pltpu.CompilerParams(vmem_limit_bytes=MIB, has_side_effects=True),
    )(weights.table, weights.w)
    return dict(zip(places, results))


def gained(x_ref, gain_ref, place, tab):
    wide = x_ref[...].astype(jnp.float32)
    square = wide * wide
    total = square[:, :LANE]
    for i in range(1, square.shape[1] // LANE):
        total = total + square[:, i * LANE : (i + 1) * LANE]
    return (wide * gain_ref[tab[place]]).astype(jnp.bfloat16), total


def add_products(x_refs, weight_of, acc_in, acc, branches, looped):
    channels = x_refs[0].shape[-1]
    block = min(512, channels)

    def branch(b):
        weights = [weight_of(k, b) for k in range(len(x_refs))]
        for i in range(channels // block):
            cols = pl.ds(i * block, block)
            total = None if acc_in is None else acc_in[b, :, cols]
            for x, w in zip(x_refs, weights):
                part = jnp.dot(x[...], w[:, cols], preferred_element_type=jnp.float32)
                total = part if total is None else total + part
            acc[b, :, cols] = total

    if looped:
        pl.loop(0, branches)(branch)
    else:
        for b in range(branches):
            branch(b)


def in_body(first, looped, tab, places, x_refs, weight_of, in_refs, out_refs, scratch):
    gain_ref = in_refs[0]
    acc_in, total = (None, None) if first else (in_refs[1], in_refs[2][...])
    acc, ssq = out_refs
    xs = [scratch[0].at[k] for k in range(len(places))]
    for x_ref, x, place in zip(x_refs, xs, places):
        x[...], square = gained(x_ref, gain_ref, place, tab)
        total = square if total is None else total + square
    ssq[...] = total
    add_products(xs, weight_of, acc_in, acc, BRANCHES, looped)


def in_chunk(weights, gain, pieces, carry, ahead=()):
    filling = bool(weights.places - weights.kept.keys())
    tokens, channels = pieces[0][1].shape
    first = carry is None
    return product_call(
        functools.partial(in_body, first, filling or len(pieces) != 2),
        weights,
        pieces,
        [gain] + ([] if first else list(carry)),
        [
            jax.ShapeDtypeStruct((BRANCHES, tokens, channels), jnp.float32),
            jax.ShapeDtypeStruct((tokens, LANE), jnp.float32),
        ],
        {} if first else {1: 0, 2: 1},
        [pltpu.VMEM((len(pieces), tokens, channels), jnp.bfloat16)],
        2.5,
        0,
        ahead if filling else (),
    )


def add_taps(sums, strip_at, taps, cols, reach):
    count = len(sums)
    for rest in range(STRIP):
        held = {}
        for m in range(count - 1, -1, -1):
            uses = [a for a in range(count) if 0 <= STRIP * (a - m) + rest < reach]
            if not uses:
                continue
            rows = strip_at(STRIP * m - rest)
            for a in uses:
                j = STRIP * (a - m) + rest
                if j not in held:
                    held[j] = taps[pl.ds(j, 1), cols]
                sums[a] += held[j] * rows


def mix_body(width, turn_at, looped, tab, places, x_refs, weight_of, in_refs, out_refs, scratch):
    gain_ref, acc_in, ssq_in, sfilt, taps, cached, tails = in_refs[:7]
    mine = tab[turn_at] != 0
    mixed, proj, prod = out_refs
    acc, xg, ext, pz = scratch
    tokens, channels = mixed.shape
    appended = tokens // REQUESTS
    xs = [xg.at[k] for k in range(len(places))]
    total = ssq_in[...]
    for x_ref, x, place in zip(x_refs, xs, places):
        x[...], square = gained(x_ref, gain_ref, place, tab)
        total = total + square
    add_products(xs, weight_of, acc_in, acc, BRANCHES, looped)
    scale = lax.rsqrt(jnp.sum(total, axis=1, keepdims=True) / width + EPS)
    for b in range(BRANCHES):
        projected = (acc[b] * scale).astype(jnp.bfloat16)

        @pl.when(mine)
        def _(b=b, projected=projected):
            proj[b] = projected

        wide = projected.astype(jnp.float32)
        for r in range(REQUESTS):
            ext[b, r, :TAIL] = tails[r, b]
            ext[b, r, TAIL:] = wide[r * appended : (r + 1) * appended]
    pz[:appended] = jnp.zeros((appended, channels), jnp.float32)
    block = min(256, channels)
    short = sfilt.shape[0] // BRANCHES

    @pl.loop(0, REQUESTS)
    def _(r):
        rows = pl.ds(pl.multiple_of(r * appended, appended), appended)

        @pl.loop(0, channels // block)
        def _(i):
            cols = pl.ds(pl.multiple_of(i * block, block), block)
            branches = []
            for b in range(BRANCHES):
                total = jnp.zeros((appended, block), jnp.float32)
                for j in range(short):
                    total = total + sfilt[j * BRANCHES + b, :, cols] * ext[b, r, pl.ds(TAIL - j, appended), cols]
                branches.append(total)
            product = (branches[1] * branches[2]).astype(jnp.bfloat16)
            pz[pl.ds(appended, appended), cols] = product.astype(jnp.float32)

            @pl.when(mine)
            def _():
                prod[rows, cols] = product

            sums = [cached[r, pl.ds(at, STRIP), cols] for at in range(0, appended, STRIP)]
            add_taps(sums, lambda at: pz[pl.ds(appended + at, STRIP), cols], taps, cols, min(appended, LONG))
            mixed[rows, cols] = (branches[0] * jnp.concatenate(sums, axis=0)).astype(jnp.bfloat16)


def mix(weights, gain, width, turn_at, pieces, carry, sfilt, taps, cached, tails, proj, prod):
    tokens, channels = pieces[0][1].shape
    appended = tokens // REQUESTS
    return product_call(
        functools.partial(mix_body, width, turn_at, bool(weights.places - weights.kept.keys())),
        weights,
        pieces,
        [gain, *carry, sfilt, taps, cached, tails, proj, prod],
        [
            jax.ShapeDtypeStruct((tokens, channels), jnp.bfloat16),
            jax.ShapeDtypeStruct((BRANCHES, tokens, channels), jnp.bfloat16),
            jax.ShapeDtypeStruct((tokens, channels), jnp.bfloat16),
        ],
        {7: 1, 8: 2},
        [
            pltpu.VMEM((BRANCHES, tokens, channels), jnp.float32),
            pltpu.VMEM((len(pieces), tokens, channels), jnp.bfloat16),
            pltpu.VMEM((BRANCHES, REQUESTS, TAIL + appended, channels), jnp.float32),
            pltpu.VMEM((2 * appended, channels), jnp.float32),
        ],
        5,
        80 * tokens * channels,
    )


def out_body(first, last, turn_at, tab, places, x_refs, weight_of, in_refs, out_refs, scratch):
    acc_in = None if first else in_refs[0]
    acc = scratch[0] if last else out_refs[0]
    add_products(x_refs, weight_of, acc_in, acc, 1, False)
    if last:
        rows = (in_refs[1][...].astype(jnp.float32) + acc[0]).astype(jnp.bfloat16)
        for turn, earlier in enumerate(in_refs[2:]):
            rows = jnp.where(tab[turn_at + turn] != 0, earlier[...], rows)
        out_refs[0][...] = rows


def out_chunk(weights, pieces, acc, ahead=(), last=None, turn_at=None):
    extra = ()
    if acc is None:
        for p in [p for p in weights.kept if p not in weights.places]:
            weights.kept.pop(p)
        extra = [p for p in range(2 * weights.lanes) if p not in weights.kept and p != pieces[0][0]]
    tokens, channels = pieces[0][1].shape
    first = acc is None
    wide = jax.ShapeDtypeStruct((1, tokens, channels), jnp.float32)
    slim = jax.ShapeDtypeStruct((tokens, channels), jnp.bfloat16)
    return product_call(
        functools.partial(out_body, first, last is not None, turn_at),
        weights,
        pieces,
        ([] if first else [acc]) + ([] if last is None else list(last)),
        [wide] if last is None else [slim],
        {0: 0} if last is None and not first else {},
        [] if last is None else [pltpu.VMEM((1, tokens, channels), jnp.float32)],
        2.5,
        0,
        extra,
    )[0]


def prep_kernel(lens, short_hbm, long_hbm, taps, cached, tails, short, long, ring, sem):
    copies = [
        pltpu.make_async_copy(long_hbm, long, sem.at[0]),
        pltpu.make_async_copy(short_hbm, short, sem.at[1]),
    ]
    for copy in copies:
        copy.start()
    for copy in copies:
        copy.wait()
    appended, channels = cached.shape[1:]
    block = min(256, channels)
    ring[LONG:] = jnp.zeros((appended, block), jnp.float32)

    @pl.loop(0, REQUESTS)
    def _(r):
        rows = lax.broadcasted_iota(jnp.int32, (LONG, LONG), 0) + lax.rem(lens[r], LONG)
        turn = (lax.rem(rows, LONG) == lax.broadcasted_iota(jnp.int32, (LONG, LONG), 1)).astype(jnp.bfloat16)

        @pl.loop(0, channels // block)
        def _(i):
            cols = pl.ds(pl.multiple_of(i * block, block), block)
            for b in range(BRANCHES):
                newest = jnp.dot(turn[LONG - 2 * TAIL :], short[r, b, :, cols], preferred_element_type=jnp.float32)
                tails[r, b, :, cols] = newest[TAIL:]
            ring[:LONG] = jnp.dot(turn, long[r, :, cols], preferred_element_type=jnp.float32)
            total = jnp.zeros((appended, block), jnp.float32)
            for j in range(1, LONG):
                total = total + taps[pl.ds(j, 1), cols] * ring[pl.ds(LONG - j, appended), :]
            cached[r, :, cols] = total


def prep(lens, short, long, taps, tokens):
    channels = long.shape[-1]
    appended = tokens // REQUESTS
    return pl.pallas_call(
        prep_kernel,
        in_specs=[SMEM, HBM, HBM, WHOLE],
        out_specs=[WHOLE, WHOLE],
        out_shape=[
            jax.ShapeDtypeStruct((REQUESTS, appended, channels), jnp.float32),
            jax.ShapeDtypeStruct((REQUESTS, BRANCHES, TAIL, channels), jnp.float32),
        ],
        scratch_shapes=[
            pltpu.VMEM(short.shape, short.dtype),
            pltpu.VMEM(long.shape, long.dtype),
            pltpu.VMEM((LONG + appended, min(256, channels)), jnp.float32),
            pltpu.SemaphoreType.DMA((2,)),
        ],
        cost_estimate=pl.CostEstimate(flops=256 * tokens * channels, bytes_accessed=20 * LONG * channels, transcendentals=0),
        compiler_params=pltpu.CompilerParams(vmem_limit_bytes=8 * MIB),
        name="prep",
    )(lens, short, long, taps)


def caches_kernel(lens, proj, prod, short, long, new_short, new_long):
    tokens, channels = prod.shape
    appended = tokens // REQUESTS
    block = min(256, channels)
    slots = lax.broadcasted_iota(jnp.int32, (LONG, block), 0)

    @pl.loop(0, REQUESTS)
    def _(r):
        at = lax.rem(lens[r], LONG)
        fresh = lax.rem(slots - at + LONG, LONG) < appended
        token = lax.rem(lax.broadcasted_iota(jnp.int32, (LONG, appended), 0) - at + LONG, LONG)
        place = (token == lax.broadcasted_iota(jnp.int32, (LONG, appended), 1)).astype(jnp.bfloat16)
        rows = pl.ds(pl.multiple_of(r * appended, appended), appended)

        @pl.loop(0, channels // block)
        def _(i):
            cols = pl.ds(pl.multiple_of(i * block, block), block)

            def replace(new, old):
                turned = jnp.dot(place, new, preferred_element_type=jnp.float32)
                return jnp.where(fresh, turned, old.astype(jnp.float32)).astype(jnp.bfloat16)

            for b in range(BRANCHES):
                new_short[r, b, :, cols] = replace(proj[b, rows, cols], short[r, b, :, cols])
            new_long[r, :, cols] = replace(prod[rows, cols], long[r, :, cols])


def caches(lens, proj, prod, short, long):
    channels = long.shape[-1]
    return pl.pallas_call(
        caches_kernel,
        in_specs=[SMEM] + [WHOLE] * 4,
        out_specs=[WHOLE, WHOLE],
        out_shape=[
            jax.ShapeDtypeStruct(short.shape, jnp.bfloat16),
            jax.ShapeDtypeStruct(long.shape, jnp.bfloat16),
        ],
        cost_estimate=pl.CostEstimate(
            flops=8 * LONG * channels, bytes_accessed=32 * LONG * channels, transcendentals=0
        ),
        compiler_params=pltpu.CompilerParams(vmem_limit_bytes=6 * MIB),
        name="caches",
    )(lens, proj, prod, short, long)


def local(
    token_ids,
    cached_len,
    embed,
    gain,
    w_in,
    short_filter,
    long_filter,
    w_out,
    short_cycle,
    long_cycle,
):
    def in_hbm(w):
        return pltpu.with_memory_space_constraint(w, pltpu.HBM)

    segments = lax.axis_size("segment")
    n = lax.axis_size("seq")
    lanes = n // 2
    own_tokens = token_ids.shape[0]
    tokens = own_tokens * n
    channels = embed.shape[1]
    width = gain.shape[1]
    my_segment = lax.axis_index("segment")
    me = lax.axis_index("seq")
    lane, core = me // 2, me % 2

    steps = jnp.arange(2 * lanes, dtype=jnp.int32)
    sources = 2 * mate(lane, steps // 2, lanes) + (core ^ (steps % 2))
    mine = (jnp.arange(segments, dtype=jnp.int32) == my_segment).astype(jnp.int32)
    table = jnp.concatenate([sources.astype(jnp.int32), mine])

    pair = jnp.stack([token_ids, other_core(token_ids, lanes)])
    received = [pair]
    for step in range(1, lanes):
        received.append(gather_step(pair, step, lanes))
    rows = jnp.concatenate(received, axis=0)
    place = sources[:, None] == jnp.arange(n, dtype=jnp.int32)[None, :]
    ids_all = jnp.sum(jnp.where(place[:, :, None], rows[:, None, :], 0), axis=0).reshape(tokens)
    one_hot = (ids_all[:, None] == jnp.arange(VOCAB, dtype=jnp.int32)[None, :]).astype(jnp.bfloat16)
    start_rows = jnp.dot(one_hot, embed, preferred_element_type=jnp.float32).astype(jnp.bfloat16)

    def held(order, rounds):
        return {2 * step + half for step in order[max(0, lanes - rounds) :] for half in range(2)}

    proj_in = Weights(in_hbm(jnp.transpose(w_in[0], (1, 0, 2))), table, held(list(range(lanes)), KEPT_IN))
    proj_out = Weights(in_hbm(w_out), table, held(list(range(lanes)), KEPT_OUT))
    gains = gain.reshape(n, 1, channels)
    sfilt = short_filter[0].reshape(-1, 1, channels)
    groups = long_filter.shape[2]
    spread = (jnp.arange(channels)[None, :] // (channels // groups) == jnp.arange(groups)[:, None]).astype(jnp.float32)
    taps = jnp.dot(long_filter[0], spread, precision=lax.Precision.HIGHEST)
    short_cache = jnp.transpose(short_cycle[0], (0, 2, 1, 3))
    long_cache = long_cycle[0]
    cached, tails = prep(cached_len, in_hbm(short_cache), in_hbm(long_cache), taps, tokens)

    proj = jnp.zeros((BRANCHES, tokens, channels), jnp.bfloat16)
    prod = jnp.zeros((tokens, channels), jnp.bfloat16)
    results = []
    current = start_rows
    for turn in range(segments):
        turn_at = 2 * lanes + turn
        blocks = {0: current} if turn == 0 else {}
        for step in range(len(blocks), lanes):
            if turn == 0:
                blocks[step] = gather_step(current, step, lanes)
            else:
                blocks[step] = hop_step(current, step, turn - 1, turn, lanes)
        residual = blocks[0]
        fetch = [place for place in FETCHED if place not in proj_in.places]
        if turn == 1:
            proj_in.kept.pop(1, None)
        if turn and fetch:
            proj_in.kept.update(fetched(proj_in, fetch))
        plan = far_then_near(lanes) if turn else one_by_one(lanes)
        waiting, carry = fold(blocks, lanes, functools.partial(in_chunk, proj_in, gains), plan)
        mixed, proj, prod = mix(proj_in, gains, width, turn_at, waiting, carry, sfilt, taps, cached, tails, proj, prod)
        blocks = {0: mixed}
        for step in range(1, lanes):
            blocks[step] = gather_step(mixed, step, lanes)
        waiting, acc = fold(blocks, lanes, functools.partial(out_chunk, proj_out), near_then_rest(lanes))
        if turn + 1 < segments:
            current = out_chunk(proj_out, waiting, acc, last=(residual,))
            results.append(current)
        else:
            new_short, new_long = caches(cached_len, proj, prod, short_cache, long_cache)
            result = out_chunk(proj_out, waiting, acc, last=(residual, *results), turn_at=2 * lanes)
    return result[None], jnp.transpose(new_short, (0, 2, 1, 3))[None], new_long[None]


def solution(mesh):
    in_specs = (
        P("seq"),
        P(),
        P(None, "seq"),
        P("segment", None),
        P("segment", None, None, "seq"),
        P("segment", None, None, "seq"),
        P("segment", None, "seq"),
        P("segment", None, "seq"),
        P("segment", None, None, None, "seq"),
        P("segment", None, None, "seq"),
    )
    out_specs = (
        P("segment", None, "seq"),
        P("segment", None, None, None, "seq"),
        P("segment", None, None, "seq"),
    )
    return jax.shard_map(local, mesh=mesh, in_specs=in_specs, out_specs=out_specs, check_vma=False)
```
